32 devices in a mesh: surf: 8 (over y, x, core), norm: 4 (over z).
Axes of the slice: x: 2, y: 2, z: 4, core: 2. Of those that a mesh axis runs over, the one named last changes fastest.
Arguments:
- mode_shapes: bfloat16 [128, 64, 3, 256], P('surf'), may hold values from -6 to 6
- amplitude: float32 [128], replicated, may hold values from -0.046875 to 0.046875
- mode_patch: int32 [128], replicated, may hold values from 0 to 3
- column_patch: int32 [64, 256], replicated, may hold values from 0 to 3
- wall_mask: int32 [64, 256], P('surf'), may hold values 0 or 1
- offsets: int32 [64, 256], P('surf'), may hold values from 0 to 127
- coupling: float32 [64, 64, 256], P('norm', 'surf'), may hold values from 0.5 to 2
- pivot_inv: float32 [64, 64, 9, 256], P('norm', 'surf'), may hold values from -2 to 2
- stiffness: float32 [64, 64, 256], P('norm', 'surf'), may hold values from 0.00021972656 to 0.0005126953
Outputs:
- displacement: float32 [64, 64, 3, 256], P('norm', 'surf')
The draws below stay inside these ranges and needn't reach their ends.
All inputs are finite; a program needn't handle non-finite values. No bound on the sum of `wall_mask` on one device may be relied on, other than what follows from the above.
Results may differ from the reference program's by a relative error of at most 0.0006.
Values may be sent and summed in bfloat16 or wider, within the bound.
A program may use at most 64 MiB of HBM per device.

```python
import math
import jax
import jax.numpy as jnp
from jax import lax

MODES = 128
PATCHES = 4
SWEEPS = 3
SPAN_COUNT_B = 256
SPAN_COUNT_A = 64
DEPTH_COUNT = 64


def coupling_values(key):
    return jnp.exp(jax.random.uniform(key, (DEPTH_COUNT, SPAN_COUNT_A, SPAN_COUNT_B), jnp.float32, math.log(0.5), math.log(2.0)))


def draw_coupling(key, part):
    return coupling_values(jax.random.fold_in(key, 11))


def euler_rotation(angle_a, angle_b, angle_g):
    cos_a, sin_a = (jnp.cos(angle_a), jnp.sin(angle_a))
    cos_b, sin_b = (jnp.cos(angle_b), jnp.sin(angle_b))
    cos_g, sin_g = (jnp.cos(angle_g), jnp.sin(angle_g))
    return [[cos_a * cos_b * cos_g - sin_a * sin_g, -cos_a * cos_b * sin_g - sin_a * cos_g, cos_a * sin_b], [sin_a * cos_b * cos_g + cos_a * sin_g, -sin_a * cos_b * sin_g + cos_a * cos_g, sin_a * sin_b], [-sin_b * cos_g, sin_b * sin_g, cos_b]]


def draw_pivot_inv(key, part):
    links = coupling_values(jax.random.fold_in(key, 11))
    generator_seeds = jax.random.split(jax.random.fold_in(key, 23), 6)
    slow_share = 0.5
    slow_flag = jax.random.uniform(generator_seeds[0], (SPAN_COUNT_A, 3, SPAN_COUNT_B), jnp.float32) < slow_share
    base_gap = jnp.where(slow_flag, 0.5 / DEPTH_COUNT, 0.05)
    roughness = jax.random.uniform(generator_seeds[1], (DEPTH_COUNT, SPAN_COUNT_A, 3, SPAN_COUNT_B), jnp.float32, 0.5, 1.5)
    damping_ratio = 1.0 - base_gap[None] * roughness
    pulse_hit_share = jax.random.randint(generator_seeds[2], (DEPTH_COUNT, SPAN_COUNT_A, 1, SPAN_COUNT_B), 0, DEPTH_COUNT) < 2
    pulse_keep_share = jax.random.uniform(generator_seeds[3], (DEPTH_COUNT, SPAN_COUNT_A, 1, SPAN_COUNT_B), jnp.float32, 0.5, 0.8)
    damping_ratio = damping_ratio * jnp.where(pulse_hit_share, pulse_keep_share, 1.0)
    angles = jax.random.uniform(generator_seeds[4], (3, SPAN_COUNT_A, SPAN_COUNT_B), jnp.float32, -math.pi, math.pi)
    rotation = euler_rotation(angles[0], angles[1], angles[2])
    turn_angles = jax.random.uniform(generator_seeds[5], (3, DEPTH_COUNT, SPAN_COUNT_A, SPAN_COUNT_B), jnp.float32, -0.06, 0.06)
    turning = euler_rotation(turn_angles[0], turn_angles[1], turn_angles[2])
    symmetric = []
    for row_index in range(3):
        symmetric_row = []
        for col_index in range(3):
            value = jnp.zeros((DEPTH_COUNT, SPAN_COUNT_A, SPAN_COUNT_B), jnp.float32)
            for inner_index in range(3):
                value = value + rotation[row_index][inner_index][None] * damping_ratio[:, :, inner_index, :] * rotation[col_index][inner_index][None]
            symmetric_row.append(value)
        symmetric.append(symmetric_row)
    entries = []
    for row_index in range(3):
        for col_index in range(3):
            value = jnp.zeros((DEPTH_COUNT, SPAN_COUNT_A, SPAN_COUNT_B), jnp.float32)
            for inner_index in range(3):
                value = value + symmetric[row_index][inner_index] * turning[inner_index][col_index]
            entries.append(value / links)
    return jnp.stack(entries, axis=2)


def plant(result, stream_key, low, largest):
    longest = result.shape.index(max(result.shape))
    spots = []
    for shift in (0, 1):
        where = [jax.random.randint(jax.random.fold_in(stream_key, axis), (), 0, length) for axis, length in enumerate(result.shape)]
        where[longest] = (where[longest] + shift) % result.shape[longest]
        spots.append(tuple(where))
    return result.at[spots[0]].set(low).at[spots[1]].set(largest)


def levels(key, dims, shards, smallest, high):
    def one(position, shards_of):
        heights = jax.random.uniform(jax.random.fold_in(jax.random.fold_in(key, 6), position), (shards_of,), jnp.float32, smallest / len(shards), high / len(shards))
        return jnp.repeat(jnp.exp(heights), dims[position] // shards_of).reshape((-1,) + (1,) * (len(dims) - position - 1))

    factor_of = one(*shards[0])
    for cut in shards[1:]:
        factor_of = factor_of * one(*cut)
    return factor_of


def noise(own_key, shape, scale, limit, cuts=(), kind=jnp.bfloat16):
    result = scale * jax.random.normal(own_key, shape, jnp.float32)
    if cuts:
        result = result * levels(own_key, shape, cuts, -0.22, 0.18)
    return jnp.clip(result, -limit, limit).astype(kind)


def setup_inputs(seed: int = 0) -> dict:
    splits = jax.random.split(jax.random.key(seed), 10)
    mode_shapes = noise(splits[0], (MODES, SPAN_COUNT_A, 3, SPAN_COUNT_B), 1.0, 6.0, ((0, 8),))
    amplitude = noise(splits[1], (MODES,), (0.5 / DEPTH_COUNT), 0.046875, (), jnp.float32)
    mode_patch = plant(jax.random.randint(splits[2], (MODES,), 0, PATCHES), jax.random.fold_in(splits[2], 1), 0, PATCHES - 1).astype(jnp.int32)
    column_patch = plant(jax.random.randint(splits[3], (SPAN_COUNT_A, SPAN_COUNT_B), 0, PATCHES), jax.random.fold_in(splits[3], 1), 0, PATCHES - 1).astype(jnp.int32)
    wall_mask = plant((jax.random.randint(splits[4], (SPAN_COUNT_A, SPAN_COUNT_B), 0, 4) < 3).astype(jnp.int32), jax.random.fold_in(splits[4], 1), 0, 1)
    offsets = plant(jax.random.randint(splits[5], (SPAN_COUNT_A, SPAN_COUNT_B), 0, 2 * DEPTH_COUNT), jax.random.fold_in(splits[5], 1), 0, (2 * DEPTH_COUNT) - 1).astype(jnp.int32)
    coupling = draw_coupling(jax.random.fold_in(splits[9], 71), 0)
    pivot_inv = draw_pivot_inv(jax.random.fold_in(splits[9], 71), 0)
    stiffness = jnp.clip(jnp.exp(math.log(0.0005126953) - 0.84729784 * jax.random.uniform(splits[8], (DEPTH_COUNT, SPAN_COUNT_A, SPAN_COUNT_B), jnp.float32) ** levels(splits[8], (DEPTH_COUNT, SPAN_COUNT_A, SPAN_COUNT_B), ((0, 4), (1, 8)), -0.2, 0.2)), 0.00021972656, 0.0005126953)
    return dict(mode_shapes=mode_shapes, amplitude=amplitude, mode_patch=mode_patch, column_patch=column_patch, wall_mask=wall_mask, offsets=offsets, coupling=coupling, pivot_inv=pivot_inv, stiffness=stiffness)


def mat_vec(matrix, vector):
    blocks = matrix.reshape(matrix.shape[:-2] + (3, 3, matrix.shape[-1]))
    return jnp.sum(blocks * vector[..., None, :, :], axis=-2)


def forward(pivots, lower_link, right_side, inflow):
    def advance(state_now, layer_data):
        pivot_block, link_row, source_row = layer_data
        updated = mat_vec(pivot_block, source_row + link_row[:, None, :] * state_now)
        return updated, updated

    last_value, forward_values = lax.scan(advance, inflow, (pivots, lower_link, right_side))
    return forward_values, last_value


def backward(pivots, upper_link, forward_values, outflow):
    def advance(state_now, layer_data):
        pivot_block, link_row, value_row = layer_data
        updated = value_row + mat_vec(pivot_block, link_row[:, None, :] * state_now)
        return updated, updated

    first_value, solved = lax.scan(advance, outflow, (pivots, upper_link, forward_values), reverse=True)
    return solved, first_value


def neighbours(displaced):
    zero_column = jnp.zeros_like(displaced[..., :1])
    neighbour_sum = jnp.roll(displaced, 1, axis=1) + jnp.roll(displaced, -1, axis=1)
    neighbour_sum = neighbour_sum + jnp.concatenate([displaced[..., 1:], zero_column], axis=-1)
    return neighbour_sum + jnp.concatenate([zero_column, displaced[..., :-1]], axis=-1)


def reference(mode_shapes, amplitude, mode_patch, column_patch, wall_mask, offsets, coupling, pivot_inv, stiffness):
    select = (mode_patch[:, None, None] == column_patch[None]).astype(jnp.float32)
    weights = amplitude[:, None, None] * select
    wall_shift = jnp.einsum("mij,micj->icj", weights, mode_shapes.astype(jnp.float32))
    wall_shift = wall_shift * wall_mask[:, None, :].astype(jnp.float32)
    depth_index = jnp.arange(DEPTH_COUNT, dtype=jnp.int32)
    lower_link = jnp.where(depth_index[:, None, None] == offsets[None], jnp.zeros_like(coupling), coupling)
    upper_link = jnp.concatenate([lower_link[1:], jnp.zeros_like(lower_link[:1])], axis=0)
    blend_weight = 1.0 - depth_index.astype(jnp.float32) / DEPTH_COUNT
    displaced = blend_weight[:, None, None, None] * wall_shift[None]
    wall_term = lower_link[0][:, None, :] * wall_shift
    zero_state = jnp.zeros((SPAN_COUNT_A, 3, SPAN_COUNT_B), jnp.float32)
    for sweep_index in range(SWEEPS):
        right_side = stiffness[:, :, None, :] * neighbours(displaced)
        right_side = right_side.at[0].add(wall_term)
        forward_values = forward(pivot_inv, lower_link, right_side, zero_state)[0]
        displaced = backward(pivot_inv, upper_link, forward_values, zero_state)[0]
    return displaced
```

```python
import functools

import jax
import jax.numpy as jnp
from jax import lax
from jax.experimental import pallas as pl
from jax.experimental.pallas import tpu as pltpu
from jax.sharding import PartitionSpec as P

SWEEPS = 3
MESH = pl.DeviceIdType.MESH


def loop(count, body, init, unroll=4):
    if count % unroll:
        unroll = 1

    def outer(step, carry):
        for part in range(unroll):
            carry = body(step * unroll + part, carry)
        return carry

    return lax.fori_loop(0, count // unroll, outer, init)


def mat_vec(matrix, vector):
    return [
        matrix[3 * a] * vector[0] + matrix[3 * a + 1] * vector[1] + matrix[3 * a + 2] * vector[2]
        for a in range(3)
    ]


def mat_mat(left, right):
    return [
        left[3 * a] * right[b] + left[3 * a + 1] * right[3 + b] + left[3 * a + 2] * right[6 + b]
        for a in range(3)
        for b in range(3)
    ]


def added(left, right):
    return [a + b for a, b in zip(left, right)]


def planes(ref, index, count=3):
    return [ref[index, c] for c in range(count)]


def put(ref, index, values):
    for c, value in enumerate(values):
        ref[index, c] = value


def kernel(
    surf_size,
    norm_size,
    amplitude,
    mode_patch,
    column_patch,
    wall_mask,
    offsets,
    modes_hbm,
    coupling_hbm,
    pivot_hbm,
    stiffness_hbm,
    out,
    modes,
    coupling,
    pivot,
    stiffness,
    link,
    link_next,
    maps,
    end_map,
    part,
    got,
    mask_edge,
    wall,
    values,
    edge,
    edge_out,
    edge_in,
    halo,
    f_in,
    f_out,
    o_in,
    o_out,
    o_true,
    h_in,
    h_out,
    load_sem,
    part_send,
    part_recv,
    mask_send,
    mask_recv,
    link_send,
    link_recv,
    h_send,
    h_recv,
    f_send,
    f_recv,
    o_send,
    o_recv,
    edge_send,
    edge_recv,
):
    S, N = surf_size, norm_size
    half = N // 2
    K, _, R, W = pivot.shape
    M = modes.shape[0]
    B = 2 * R
    blocks = modes.shape[2] // B
    me = lax.axis_index("surf")
    place = lax.axis_index("norm")
    before = lax.rem(me + S - 1, S)
    after = lax.rem(me + 1, S)
    first, last = place == 0, place == N - 1

    def to_surf(src, dst, send, recv, target):
        return pltpu.make_async_remote_copy(
            src_ref=src, dst_ref=dst, send_sem=send, recv_sem=recv,
            device_id={"surf": target}, device_id_type=MESH,
        )

    def to_norm(src, dst, send, recv, target):
        return pltpu.make_async_remote_copy(
            src_ref=src, dst_ref=dst, send_sem=send, recv_sem=recv,
            device_id={"norm": target}, device_id_type=MESH,
        )

    mode_loads = [
        pltpu.make_async_copy(
            modes_hbm.at[:, :, pl.ds(b * B, B), :], modes.at[:, :, pl.ds(b * B, B), :], load_sem.at[3 + b]
        )
        for b in range(blocks)
    ]
    loads = [
        pltpu.make_async_copy(coupling_hbm, coupling, load_sem.at[0]),
        pltpu.make_async_copy(pivot_hbm, pivot, load_sem.at[1]),
        pltpu.make_async_copy(stiffness_hbm, stiffness, load_sem.at[2]),
    ]
    for copy in mode_loads + loads:
        copy.start()

    barrier = pltpu.get_barrier_semaphore()
    for hop in range(1, S):
        pl.semaphore_signal(
            barrier, inc=1, device_id={"surf": lax.rem(me + hop, S)}, device_id_type=MESH
        )

    @pl.when(jnp.logical_not(first))
    def _():
        pl.semaphore_signal(barrier, inc=1, device_id={"norm": place - 1}, device_id_type=MESH)

    @pl.when(jnp.logical_not(last))
    def _():
        pl.semaphore_signal(barrier, inc=1, device_id={"norm": place + 1}, device_id_type=MESH)

    own_mode = me * M
    for b in range(blocks):
        mode_loads[b].wait()
        patch = column_patch[b * B : (b + 1) * B, :]

        def mode_step(m, sums):
            weight = jnp.where(
                patch == mode_patch[own_mode + m], amplitude[own_mode + m], jnp.float32(0)
            )
            return [
                sums[c] + weight * modes[m, c, b * B : (b + 1) * B, :].astype(jnp.float32)
                for c in range(3)
            ]

        sums = loop(M, mode_step, [jnp.zeros((B, W), jnp.float32)] * 3)
        for c in range(3):
            for side in range(2):
                dest = 2 * b + side
                block = sums[c][side * R : (side + 1) * R]
                part[dest, c] = block
                part[(dest + 1) % S, 3, c : c + 1, :] = block[R - 1 : R]
                part[(dest - 1) % S, 3, 3 + c : 4 + c, :] = block[0:1]

    @pl.when(jnp.logical_or(first, last))
    def _():
        pl.semaphore_wait(barrier, S)

    @pl.when(jnp.logical_not(jnp.logical_or(first, last)))
    def _():
        pl.semaphore_wait(barrier, S + 1)

    def part_copy(hop):
        dest = lax.rem(me + hop, S)
        return to_surf(part.at[dest], got.at[hop], part_send.at[hop], part_recv.at[hop], dest)

    for hop in range(1, S):
        part_copy(hop).start()
    mask_up = to_surf(wall_mask, mask_edge.at[0], mask_send.at[0], mask_recv.at[0], after)
    mask_down = to_surf(wall_mask, mask_edge.at[1], mask_send.at[1], mask_recv.at[1], before)
    mask_up.start()
    mask_down.start()
    link_copy = to_norm(coupling_hbm.at[0], link_next, link_send, link_recv, place - 1)

    @pl.when(jnp.logical_not(first))
    def _():
        link_copy.start()

    for copy in loads:
        copy.wait()
    cut = offsets[...]
    base = place * K

    def link_step(k, carry):
        link[k] = jnp.where(cut == base + k, jnp.float32(0), coupling[k])
        return carry

    loop(K, link_step, 0)

    @pl.when(last)
    def _():
        link[K] = jnp.zeros((R, W), jnp.float32)

    def lower_step(k, state):
        scaled = [p * link[k] for p in planes(pivot, k, 9)]
        state = mat_mat(scaled, state)
        put(maps, k, state)
        return state

    first_map = [p * link[0] for p in planes(pivot, 0, 9)]
    put(maps, 0, first_map)
    ends = lax.fori_loop(1, K, lower_step, first_map)
    for c in range(9):
        end_map[c] = ends[c]

    @pl.when(jnp.logical_not(last))
    def _():
        link_copy.wait_recv()
        link[K] = jnp.where(cut == base + K, jnp.float32(0), link_next[...])

    def upper_step(step, state):
        k = K - 1 - step
        scaled = [p * link[k + 1] for p in planes(pivot, k, 9)]
        state = added(planes(maps, k, 9), mat_mat(scaled, state[:9])) + mat_mat(scaled, state[9:])
        put(maps, k, state)
        return state

    top_link = link[K]
    top_state = planes(maps, K - 1, 9) + [p * top_link for p in planes(pivot, K - 1, 9)]
    put(maps, K - 1, top_state)
    top_state = lax.fori_loop(1, K, upper_step, top_state)

    h_copy = to_norm(h_out, h_in, h_send, h_recv, place - 1)
    gets_h = jnp.logical_and(place >= half - 1, jnp.logical_not(last))

    @pl.when(gets_h)
    def _():
        h_copy.wait_recv()

    @pl.when(jnp.logical_not(gets_h))
    def _():
        h_in[...] = jnp.zeros((9, R, W), jnp.float32)

    @pl.when(place >= half)
    def _():
        inner = mat_mat([h_in[c] for c in range(9)], [end_map[c] for c in range(9)])
        whole = added(planes(maps, 0, 9), mat_mat([maps[0, 9 + c] for c in range(9)], inner))
        for c in range(9):
            h_out[c] = whole[c]
        h_copy.start()

    @pl.when(first)
    def _():
        f_in[...] = jnp.zeros(f_in.shape, jnp.float32)

    @pl.when(last)
    def _():
        o_in[...] = jnp.zeros(o_in.shape, jnp.float32)

    total = [part[me, c] for c in range(4)]
    mask_up.wait_recv()
    mask_down.wait_recv()
    for hop in range(1, S):
        part_copy(hop).wait_recv()
        total = [total[c] + got[hop, c] for c in range(4)]
    mask = wall_mask[...].astype(jnp.float32)
    low_mask = mask_edge[0, R - 1 : R, :].astype(jnp.float32)
    high_mask = mask_edge[1, 0:1, :].astype(jnp.float32)
    row = lax.broadcasted_iota(jnp.int32, (R, W), 0)
    lane = lax.broadcasted_iota(jnp.int32, (R, W), 1)

    def around(x, low, high):
        nearby = jnp.where(row == 0, low, pltpu.roll(x, 1, 0))
        nearby += jnp.where(row == R - 1, high, pltpu.roll(x, R - 1, 0))
        nearby += jnp.where(lane == 0, jnp.float32(0), pltpu.roll(x, 1, 1))
        return nearby + jnp.where(lane == W - 1, jnp.float32(0), pltpu.roll(x, W - 1, 1))

    at_wall = jnp.where(first, jnp.float32(1), jnp.float32(0))
    for c in range(3):
        shift = total[c] * mask
        wall[c] = link[0] * shift * at_wall
        wall[3 + c] = around(
            shift, total[3][c : c + 1] * low_mask, total[3][3 + c : 4 + c] * high_mask
        )

    def edge_copies(sweep):
        return [
            to_surf(edge_out.at[sweep, 1], edge_in.at[sweep, 0], edge_send.at[sweep, 0], edge_recv.at[sweep, 0], after),
            to_surf(edge_out.at[sweep, 0], edge_in.at[sweep, 1], edge_send.at[sweep, 1], edge_recv.at[sweep, 1], before),
        ]

    def chain_copies(sweep):
        return (
            to_norm(f_out.at[sweep], f_in.at[sweep], f_send.at[sweep], f_recv.at[sweep], place + 1),
            to_norm(o_out.at[sweep], o_in.at[sweep], o_send.at[sweep], o_recv.at[sweep], place - 1),
        )

    for sweep in range(SWEEPS):
        if sweep > 0:
            for copy in edge_copies(sweep - 1):
                copy.wait_recv()
            for side in range(2):
                halo[side] = edge_in[sweep - 1, side].astype(jnp.float32)

        def source(k, sweep=sweep):
            if sweep == 0:
                blend = 1.0 - (base + k).astype(jnp.float32) / (K * N)
                factor = stiffness[k] * blend
                return [factor * wall[3 + c] for c in range(3)]
            return [
                stiffness[k]
                * around(out[k, c], halo[0, c, pl.ds(k, 1), :], halo[1, c, pl.ds(k, 1), :])
                for c in range(3)
            ]

        def forward(k, state):
            right = added(source(k), [link[k] * s for s in state])
            state = mat_vec(planes(pivot, k, 9), right)
            put(values, k, state)
            return state

        start = mat_vec(
            planes(pivot, 0, 9), added(source(0), [wall[c] for c in range(3)])
        )
        put(values, 0, start)
        ends = lax.fori_loop(1, K, forward, start)

        def backward(step, state):
            k = K - 1 - step
            state = added(
                planes(values, k), mat_vec(planes(pivot, k, 9), [link[k + 1] * s for s in state])
            )
            put(values, k, state)
            return state

        tops = lax.fori_loop(1, K, backward, ends)
        for c in range(3):
            edge[0, c] = ends[c]
            edge[1, c] = tops[c]

        f_copy, o_copy = chain_copies(sweep)

        def own(which):
            return [edge[which, c] for c in range(3)]

        def end_state(entering):
            return added(own(0), mat_vec([end_map[c] for c in range(9)], entering))

        def leaving(state):
            return added(
                planes(o_in, sweep), mat_vec([h_in[c] for c in range(9)], state)
            )

        @pl.when(place < half)
        def _():
            @pl.when(jnp.logical_not(first))
            def _():
                f_copy.wait_recv()

            entering = planes(f_in, sweep)
            state = end_state(entering)
            put(f_out, sweep, state)
            f_copy.start()
            o_copy.wait_recv()
            above = leaving(state)
            for c in range(3):
                o_true[c] = above[c]

            @pl.when(jnp.logical_not(first))
            def _():
                top = added(own(1), mat_vec([maps[0, c] for c in range(9)], entering))
                top = added(top, mat_vec([maps[0, 9 + c] for c in range(9)], above))
                put(o_out, sweep, top)
                o_copy.start()

        @pl.when(place >= half)
        def _():
            @pl.when(jnp.logical_not(last))
            def _():
                o_copy.wait_recv()

            top = added(
                own(1), mat_vec([maps[0, 9 + c] for c in range(9)], leaving(own(0)))
            )
            put(o_out, sweep, top)
            o_copy.start()
            f_copy.wait_recv()
            state = end_state(planes(f_in, sweep))

            @pl.when(jnp.logical_not(last))
            def _():
                put(f_out, sweep, state)
                f_copy.start()

            above = leaving(state)
            for c in range(3):
                o_true[c] = above[c]

        entering = planes(f_in, sweep)
        above = [o_true[c] for c in range(3)]

        def finish(k, carry, sweep=sweep):
            state = added(planes(values, k), mat_vec(planes(maps, k, 9), entering))
            state = added(state, mat_vec([maps[k, 9 + c] for c in range(9)], above))
            put(out, k, state)
            if sweep < SWEEPS - 1:
                for c in range(3):
                    halo[0, c, pl.ds(k, 1), :] = state[c][0:1]
                    halo[1, c, pl.ds(k, 1), :] = state[c][R - 1 : R]
            return carry

        loop(K, finish, 0, 2)
        if sweep < SWEEPS - 1:
            for side in range(2):
                edge_out[sweep, side] = halo[side].astype(jnp.bfloat16)
            for copy in edge_copies(sweep):
                copy.start()

    for hop in range(1, S):
        part_copy(hop).wait_send()
    mask_up.wait_send()
    mask_down.wait_send()
    for sweep in range(SWEEPS - 1):
        for copy in edge_copies(sweep):
            copy.wait_send()

    @pl.when(place >= half)
    def _():
        h_copy.wait_send()

    @pl.when(jnp.logical_not(first))
    def _():
        link_copy.wait_send()
        for sweep in range(SWEEPS):
            chain_copies(sweep)[1].wait_send()

    @pl.when(jnp.logical_not(last))
    def _():
        for sweep in range(SWEEPS):
            chain_copies(sweep)[0].wait_send()


def per_device(
    surf_size, norm_size, mode_shapes, amplitude, mode_patch, column_patch, wall_mask, offsets,
    coupling, pivot_inv, stiffness,
):
    S = surf_size
    modes = mode_shapes.transpose(0, 2, 1, 3)
    pivot = pivot_inv.transpose(0, 2, 1, 3)
    K, _, R, W = pivot.shape
    f32, bf16 = jnp.float32, jnp.bfloat16
    vmem = pl.BlockSpec(memory_space=pltpu.VMEM)
    smem = pl.BlockSpec(memory_space=pltpu.SMEM)
    hbm = pl.BlockSpec(memory_space=pl.ANY)
    dma = pltpu.SemaphoreType.DMA
    out = pl.pallas_call(
        functools.partial(kernel, surf_size, norm_size),
        out_shape=jax.ShapeDtypeStruct((K, 3, R, W), f32),
        in_specs=[smem, smem, vmem, vmem, vmem, hbm, hbm, hbm, hbm],
        out_specs=vmem,
        scratch_shapes=[
            pltpu.VMEM(modes.shape, bf16),
            pltpu.VMEM((K, R, W), f32),
            pltpu.VMEM((K, 9, R, W), f32),
            pltpu.VMEM((K, R, W), f32),
            pltpu.VMEM((K + 1, R, W), f32),
            pltpu.VMEM((R, W), f32),
            pltpu.VMEM((K, 18, R, W), f32),
            pltpu.VMEM((9, R, W), f32),
            pltpu.VMEM((S, 4, R, W), f32),
            pltpu.VMEM((S, 4, R, W), f32),
            pltpu.VMEM((2, R, W), jnp.int32),
            pltpu.VMEM((6, R, W), f32),
            pltpu.VMEM((K, 3, R, W), f32),
            pltpu.VMEM((2, 3, R, W), f32),
            pltpu.VMEM((SWEEPS - 1, 2, 3, K, W), bf16),
            pltpu.VMEM((SWEEPS - 1, 2, 3, K, W), bf16),
            pltpu.VMEM((2, 3, K, W), f32),
            pltpu.VMEM((SWEEPS, 3, R, W), f32),
            pltpu.VMEM((SWEEPS, 3, R, W), f32),
            pltpu.VMEM((SWEEPS, 3, R, W), f32),
            pltpu.VMEM((SWEEPS, 3, R, W), f32),
            pltpu.VMEM((3, R, W), f32),
            pltpu.VMEM((9, R, W), f32),
            pltpu.VMEM((9, R, W), f32),
            dma((3 + modes.shape[2] // (2 * R),)),
            dma((S,)),
            dma((S,)),
            dma((2,)),
            dma((2,)),
            dma,
            dma,
            dma,
            dma,
            dma((SWEEPS,)),
            dma((SWEEPS,)),
            dma((SWEEPS,)),
            dma((SWEEPS,)),
            dma((SWEEPS - 1, 2)),
            dma((SWEEPS - 1, 2)),
        ],
        compiler_params=pltpu.CompilerParams(collective_id=0, has_side_effects=True),
        name="line_sweeps",
    )(amplitude, mode_patch, column_patch, wall_mask, offsets, modes, coupling, pivot, stiffness)
    return out.transpose(0, 2, 1, 3)


def solution(mesh):
    return jax.shard_map(
        functools.partial(per_device, mesh.shape["surf"], mesh.shape["norm"]),
        mesh=mesh,
        in_specs=(
            P("surf", None, None, None),
            P(),
            P(),
            P(),
            P("surf", None),
            P("surf", None),
            P("norm", "surf", None),
            P("norm", "surf", None, None),
            P("norm", "surf", None),
        ),
        out_specs=P("norm", "surf", None, None),
        check_vma=False,
    )
```

```python
import functools

import jax
import jax.numpy as jnp
from jax import lax
from jax.experimental import pallas as pl
from jax.experimental.pallas import tpu as pltpu
from jax.sharding import PartitionSpec as P

SWEEPS = 3
MESH = pl.DeviceIdType.MESH


def loop(count, body, init, unroll=4):
    if count % unroll:
        unroll = 1

    def outer(step, carry):
        for part in range(unroll):
            carry = body(step * unroll + part, carry)
        return carry

    return lax.fori_loop(0, count // unroll, outer, init)


def mat_vec(matrix, vector):
    return [
        matrix[3 * a] * vector[0] + matrix[3 * a + 1] * vector[1] + matrix[3 * a + 2] * vector[2]
        for a in range(3)
    ]


def mat_mat(left, right):
    return [
        left[3 * a] * right[b] + left[3 * a + 1] * right[3 + b] + left[3 * a + 2] * right[6 + b]
        for a in range(3)
        for b in range(3)
    ]


def added(left, right):
    return [a + b for a, b in zip(left, right)]


def planes(ref, index, count=3):
    return [ref[index, c] for c in range(count)]


def put(ref, index, values):
    for c, value in enumerate(values):
        ref[index, c] = value


def kernel(
    surf_size,
    norm_size,
    amplitude,
    mode_patch,
    column_patch,
    wall_mask,
    offsets,
    modes_hbm,
    coupling_hbm,
    pivot_hbm,
    stiffness_hbm,
    out,
    modes,
    coupling,
    pivot,
    stiffness,
    link,
    link_next,
    maps,
    end_map,
    part,
    got,
    mask_edge,
    wall,
    values,
    enter,
    edge_out,
    edge_in,
    halo,
    f_in,
    f_out,
    o_in,
    o_out,
    h_in,
    h_out,
    up_in,
    up_out,
    down_in,
    down_out,
    load_sem,
    part_send,
    part_recv,
    mask_send,
    mask_recv,
    link_send,
    link_recv,
    h_send,
    h_recv,
    up_send,
    up_recv,
    down_send,
    down_recv,
    f_send,
    f_recv,
    o_send,
    o_recv,
    edge_send,
    edge_recv,
):
    S, N = surf_size, norm_size
    K, _, R, W = pivot.shape
    M = modes.shape[0]
    B = 2 * R
    blocks = modes.shape[2] // B
    me = lax.axis_index("surf")
    place = lax.axis_index("norm")
    before = lax.rem(me + S - 1, S)
    after = lax.rem(me + 1, S)
    first, last = place == 0, place == N - 1

    def to_surf(src, dst, send, recv, target):
        return pltpu.make_async_remote_copy(
            src_ref=src, dst_ref=dst, send_sem=send, recv_sem=recv,
            device_id={"surf": target}, device_id_type=MESH,
        )

    def to_norm(src, dst, send, recv, target):
        return pltpu.make_async_remote_copy(
            src_ref=src, dst_ref=dst, send_sem=send, recv_sem=recv,
            device_id={"norm": target}, device_id_type=MESH,
        )

    mode_loads = [
        pltpu.make_async_copy(
            modes_hbm.at[:, :, pl.ds(b * B, B), :], modes.at[:, :, pl.ds(b * B, B), :], load_sem.at[3 + b]
        )
        for b in range(blocks)
    ]
    loads = [
        pltpu.make_async_copy(coupling_hbm, coupling, load_sem.at[0]),
        pltpu.make_async_copy(pivot_hbm, pivot, load_sem.at[1]),
        pltpu.make_async_copy(stiffness_hbm, stiffness, load_sem.at[2]),
    ]
    for copy in mode_loads + loads:
        copy.start()

    barrier = pltpu.get_barrier_semaphore()
    for hop in range(1, S):
        pl.semaphore_signal(
            barrier, inc=1, device_id={"surf": lax.rem(me + hop, S)}, device_id_type=MESH
        )

    for hop in range(1, N):
        pl.semaphore_signal(
            barrier, inc=1, device_id={"norm": lax.rem(place + hop, N)}, device_id_type=MESH
        )

    own_mode = me * M
    for b in range(blocks):
        mode_loads[b].wait()
        patch = column_patch[b * B : (b + 1) * B, :]

        def mode_step(m, sums):
            weight = jnp.where(
                patch == mode_patch[own_mode + m], amplitude[own_mode + m], jnp.float32(0)
            )
            return [
                sums[c] + weight * modes[m, c, b * B : (b + 1) * B, :].astype(jnp.float32)
                for c in range(3)
            ]

        sums = loop(M, mode_step, [jnp.zeros((B, W), jnp.float32)] * 3)
        for c in range(3):
            for side in range(2):
                dest = 2 * b + side
                block = sums[c][side * R : (side + 1) * R]
                part[dest, c] = block
                part[(dest + 1) % S, 3, c : c + 1, :] = block[R - 1 : R]
                part[(dest - 1) % S, 3, 3 + c : 4 + c, :] = block[0:1]

    pl.semaphore_wait(barrier, S + N - 2)

    def part_copy(hop):
        dest = lax.rem(me + hop, S)
        return to_surf(part.at[dest], got.at[hop], part_send.at[hop], part_recv.at[hop], dest)

    for hop in range(1, S):
        part_copy(hop).start()
    mask_up = to_surf(wall_mask, mask_edge.at[0], mask_send.at[0], mask_recv.at[0], after)
    mask_down = to_surf(wall_mask, mask_edge.at[1], mask_send.at[1], mask_recv.at[1], before)
    mask_up.start()
    mask_down.start()
    link_copy = to_norm(coupling_hbm.at[0], link_next, link_send, link_recv, place - 1)

    @pl.when(jnp.logical_not(first))
    def _():
        link_copy.start()

    for copy in loads:
        copy.wait()
    cut = offsets[...]
    base = place * K

    def link_step(k, carry):
        link[k] = jnp.where(cut == base + k, jnp.float32(0), coupling[k])
        return carry

    loop(K, link_step, 0)

    @pl.when(last)
    def _():
        link[K] = jnp.zeros((R, W), jnp.float32)

    def lower_step(k, state):
        scaled = [p * link[k] for p in planes(pivot, k, 9)]
        state = mat_mat(scaled, state)
        put(maps, k, state)
        return state

    first_map = [p * link[0] for p in planes(pivot, 0, 9)]
    put(maps, 0, first_map)
    ends = lax.fori_loop(1, K, lower_step, first_map)
    for c in range(9):
        end_map[c] = ends[c]

    @pl.when(jnp.logical_not(last))
    def _():
        link_copy.wait_recv()
        link[K] = jnp.where(cut == base + K, jnp.float32(0), link_next[...])

    def upper_step(step, state):
        k = K - 1 - step
        scaled = [p * link[k + 1] for p in planes(pivot, k, 9)]
        state = added(planes(maps, k, 9), mat_mat(scaled, state[:9])) + mat_mat(scaled, state[9:])
        put(maps, k, state)
        return state

    top_link = link[K]
    top_state = planes(maps, K - 1, 9) + [p * top_link for p in planes(pivot, K - 1, 9)]
    put(maps, K - 1, top_state)
    top_state = lax.fori_loop(1, K, upper_step, top_state)

    h_copy = to_norm(h_out, h_in, h_send, h_recv, place - 1)
    inside = jnp.logical_not(jnp.logical_or(first, last))

    def up_map(j):
        return to_norm(up_out.at[j], up_in.at[j], up_send.at[j], up_recv.at[j], place + 1)

    def down_map(j):
        return to_norm(down_out.at[j], down_in.at[j], down_send.at[j], down_recv.at[j], place - 1)

    def sends_up(j):
        return jnp.logical_and(place >= j, jnp.logical_not(last))

    def sends_down(j):
        return jnp.logical_and(N - 1 - place >= j, jnp.logical_not(first))

    @pl.when(last)
    def _():
        h_in[...] = jnp.zeros((9, R, W), jnp.float32)
        for c in range(9):
            h_out[c] = maps[0, c]
        h_copy.start()

    for j in range(1, min(2, N - 1)):

        @pl.when(sends_up(j))
        def _():
            put(up_out, j, [end_map[c] for c in range(9)])
            up_map(j).start()

        @pl.when(sends_down(j))
        def _():
            put(down_out, j, [maps[0, 9 + c] for c in range(9)])
            down_map(j).start()

    @pl.when(inside)
    def _():
        h_copy.wait_recv()
        inner = mat_mat([h_in[c] for c in range(9)], [end_map[c] for c in range(9)])
        whole = added(planes(maps, 0, 9), mat_mat([maps[0, 9 + c] for c in range(9)], inner))
        for c in range(9):
            h_out[c] = whole[c]
        h_copy.start()

    for j in range(2, N):

        @pl.when(place >= j)
        def _():
            up_map(j - 1).wait_recv()

        @pl.when(N - 1 - place >= j)
        def _():
            down_map(j - 1).wait_recv()

        if j < N - 1:

            @pl.when(sends_up(j))
            def _():
                put(up_out, j, mat_mat([end_map[c] for c in range(9)], planes(up_in, j - 1, 9)))
                up_map(j).start()

            @pl.when(sends_down(j))
            def _():
                put(
                    down_out, j,
                    mat_mat([maps[0, 9 + c] for c in range(9)], planes(down_in, j - 1, 9)),
                )
                down_map(j).start()

    total = [part[me, c] for c in range(4)]
    mask_up.wait_recv()
    mask_down.wait_recv()
    for hop in range(1, S):
        part_copy(hop).wait_recv()
        total = [total[c] + got[hop, c] for c in range(4)]
    mask = wall_mask[...].astype(jnp.float32)
    low_mask = mask_edge[0, R - 1 : R, :].astype(jnp.float32)
    high_mask = mask_edge[1, 0:1, :].astype(jnp.float32)
    row = lax.broadcasted_iota(jnp.int32, (R, W), 0)
    lane = lax.broadcasted_iota(jnp.int32, (R, W), 1)

    def around(x, low, high):
        nearby = jnp.where(row == 0, low, pltpu.roll(x, 1, 0))
        nearby += jnp.where(row == R - 1, high, pltpu.roll(x, R - 1, 0))
        nearby += jnp.where(lane == 0, jnp.float32(0), pltpu.roll(x, 1, 1))
        return nearby + jnp.where(lane == W - 1, jnp.float32(0), pltpu.roll(x, W - 1, 1))

    at_wall = jnp.where(first, jnp.float32(1), jnp.float32(0))
    for c in range(3):
        shift = total[c] * mask
        wall[c] = link[0] * shift * at_wall
        wall[3 + c] = around(
            shift, total[3][c : c + 1] * low_mask, total[3][3 + c : 4 + c] * high_mask
        )

    def edge_copies(sweep):
        return [
            to_surf(edge_out.at[sweep, 1], edge_in.at[sweep, 0], edge_send.at[sweep, 0], edge_recv.at[sweep, 0], after),
            to_surf(edge_out.at[sweep, 0], edge_in.at[sweep, 1], edge_send.at[sweep, 1], edge_recv.at[sweep, 1], before),
        ]

    def up_copy(sweep, j):
        return to_norm(
            f_out.at[sweep], f_in.at[sweep, j], f_send.at[sweep, j], f_recv.at[sweep, j], place + j
        )

    def down_copy(sweep, j):
        return to_norm(
            o_out.at[sweep], o_in.at[sweep, j], o_send.at[sweep, j], o_recv.at[sweep, j], place - j
        )

    for sweep in range(SWEEPS):
        if sweep > 0:
            for copy in edge_copies(sweep - 1):
                copy.wait_recv()
            for side in range(2):
                halo[side] = edge_in[sweep - 1, side].astype(jnp.float32)

        def source(k, sweep=sweep):
            if sweep == 0:
                blend = 1.0 - (base + k).astype(jnp.float32) / (K * N)
                factor = stiffness[k] * blend
                return [factor * wall[3 + c] for c in range(3)]
            return [
                stiffness[k]
                * around(out[k, c], halo[0, c, pl.ds(k, 1), :], halo[1, c, pl.ds(k, 1), :])
                for c in range(3)
            ]

        def forward(k, state):
            right = added(source(k), [link[k] * s for s in state])
            state = mat_vec(planes(pivot, k, 9), right)
            put(values, k, state)
            return state

        start = mat_vec(
            planes(pivot, 0, 9), added(source(0), [wall[c] for c in range(3)])
        )
        put(values, 0, start)
        ends = lax.fori_loop(1, K, forward, start)

        def backward(step, state):
            k = K - 1 - step
            state = added(
                planes(values, k), mat_vec(planes(pivot, k, 9), [link[k + 1] * s for s in state])
            )
            put(values, k, state)
            return state

        tops = lax.fori_loop(1, K, backward, ends)
        put(f_out, sweep, ends)
        for j in range(N - 1, 0, -1):

            @pl.when(place + j < N)
            def _():
                up_copy(sweep, j).start()

        if sweep == 0:

            @pl.when(first)
            def _():
                h_copy.wait_recv()

        @pl.when(jnp.logical_not(first))
        def _():
            top = added(
                tops,
                mat_vec(
                    [maps[0, 9 + c] for c in range(9)], mat_vec([h_in[c] for c in range(9)], ends)
                ),
            )
            put(o_out, sweep, top)
            for j in range(N - 1, 0, -1):

                @pl.when(place - j >= 0)
                def _():
                    down_copy(sweep, j).start()

        enter[...] = jnp.zeros(enter.shape, jnp.float32)
        for j in range(1, N):

            @pl.when(place - j >= 0)
            def _():
                up_copy(sweep, j).wait_recv()
                moved = planes(f_in.at[sweep], j)
                if j > 1:
                    moved = mat_vec(planes(up_in, j - 1, 9), moved)
                put(enter, 0, added(planes(enter, 0), moved))

            @pl.when(place + j < N)
            def _():
                down_copy(sweep, j).wait_recv()
                moved = planes(o_in.at[sweep], j)
                if j > 1:
                    moved = mat_vec(planes(down_in, j - 1, 9), moved)
                put(enter, 1, added(planes(enter, 1), moved))

        entering = planes(enter, 0)
        state = added(ends, mat_vec([end_map[c] for c in range(9)], entering))
        above = added(planes(enter, 1), mat_vec([h_in[c] for c in range(9)], state))

        def finish(k, carry, sweep=sweep):
            state = added(planes(values, k), mat_vec(planes(maps, k, 9), entering))
            state = added(state, mat_vec([maps[k, 9 + c] for c in range(9)], above))
            put(out, k, state)
            if sweep < SWEEPS - 1:
                for c in range(3):
                    halo[0, c, pl.ds(k, 1), :] = state[c][0:1]
                    halo[1, c, pl.ds(k, 1), :] = state[c][R - 1 : R]
            return carry

        loop(K, finish, 0, 2)
        if sweep < SWEEPS - 1:
            for side in range(2):
                edge_out[sweep, side] = halo[side].astype(jnp.bfloat16)
            for copy in edge_copies(sweep):
                copy.start()

    for hop in range(1, S):
        part_copy(hop).wait_send()
    mask_up.wait_send()
    mask_down.wait_send()
    for sweep in range(SWEEPS - 1):
        for copy in edge_copies(sweep):
            copy.wait_send()

    @pl.when(jnp.logical_not(first))
    def _():
        link_copy.wait_send()
        h_copy.wait_send()

    for j in range(1, N):
        if j < N - 1:

            @pl.when(sends_up(j))
            def _():
                up_map(j).wait_send()

            @pl.when(sends_down(j))
            def _():
                down_map(j).wait_send()

        for sweep in range(SWEEPS):

            @pl.when(place + j < N)
            def _():
                up_copy(sweep, j).wait_send()

            @pl.when(place - j >= 0)
            def _():
                down_copy(sweep, j).wait_send()


def per_device(
    surf_size, norm_size, mode_shapes, amplitude, mode_patch, column_patch, wall_mask, offsets,
    coupling, pivot_inv, stiffness,
):
    S, N = surf_size, norm_size
    modes = mode_shapes.transpose(0, 2, 1, 3)
    pivot = pivot_inv.transpose(0, 2, 1, 3)
    K, _, R, W = pivot.shape
    f32, bf16 = jnp.float32, jnp.bfloat16
    vmem = pl.BlockSpec(memory_space=pltpu.VMEM)
    smem = pl.BlockSpec(memory_space=pltpu.SMEM)
    hbm = pl.BlockSpec(memory_space=pl.ANY)
    dma = pltpu.SemaphoreType.DMA
    out = pl.pallas_call(
        functools.partial(kernel, surf_size, norm_size),
        out_shape=jax.ShapeDtypeStruct((K, 3, R, W), f32),
        in_specs=[smem, smem, vmem, vmem, vmem, hbm, hbm, hbm, hbm],
        out_specs=vmem,
        scratch_shapes=[
            pltpu.VMEM(modes.shape, bf16),
            pltpu.VMEM((K, R, W), f32),
            pltpu.VMEM((K, 9, R, W), f32),
            pltpu.VMEM((K, R, W), f32),
            pltpu.VMEM((K + 1, R, W), f32),
            pltpu.VMEM((R, W), f32),
            pltpu.VMEM((K, 18, R, W), f32),
            pltpu.VMEM((9, R, W), f32),
            pltpu.VMEM((S, 4, R, W), f32),
            pltpu.VMEM((S, 4, R, W), f32),
            pltpu.VMEM((2, R, W), jnp.int32),
            pltpu.VMEM((6, R, W), f32),
            pltpu.VMEM((K, 3, R, W), f32),
            pltpu.VMEM((2, 3, R, W), f32),
            pltpu.VMEM((SWEEPS - 1, 2, 3, K, W), bf16),
            pltpu.VMEM((SWEEPS - 1, 2, 3, K, W), bf16),
            pltpu.VMEM((2, 3, K, W), f32),
            pltpu.VMEM((SWEEPS, N, 3, R, W), f32),
            pltpu.VMEM((SWEEPS, 3, R, W), f32),
            pltpu.VMEM((SWEEPS, N, 3, R, W), f32),
            pltpu.VMEM((SWEEPS, 3, R, W), f32),
            pltpu.VMEM((9, R, W), f32),
            pltpu.VMEM((9, R, W), f32),
            pltpu.VMEM((N, 9, R, W), f32),
            pltpu.VMEM((N, 9, R, W), f32),
            pltpu.VMEM((N, 9, R, W), f32),
            pltpu.VMEM((N, 9, R, W), f32),
            dma((3 + modes.shape[2] // (2 * R),)),
            dma((S,)),
            dma((S,)),
            dma((2,)),
            dma((2,)),
            dma,
            dma,
            dma,
            dma,
            dma((N,)),
            dma((N,)),
            dma((N,)),
            dma((N,)),
            dma((SWEEPS, N)),
            dma((SWEEPS, N)),
            dma((SWEEPS, N)),
            dma((SWEEPS, N)),
            dma((SWEEPS - 1, 2)),
            dma((SWEEPS - 1, 2)),
        ],
        compiler_params=pltpu.CompilerParams(collective_id=0, has_side_effects=True),
        name="line_sweeps",
    )(amplitude, mode_patch, column_patch, wall_mask, offsets, modes, coupling, pivot, stiffness)
    return out.transpose(0, 2, 1, 3)


def solution(mesh):
    return jax.shard_map(
        functools.partial(per_device, mesh.shape["surf"], mesh.shape["norm"]),
        mesh=mesh,
        in_specs=(
            P("surf", None, None, None),
            P(),
            P(),
            P(),
            P("surf", None),
            P("surf", None),
            P("norm", "surf", None),
            P("norm", "surf", None, None),
            P("norm", "surf", None),
        ),
        out_specs=P("norm", "surf", None, None),
        check_vma=False,
    )
```

```python
import functools

import jax
import jax.numpy as jnp
from jax import lax
from jax.experimental import pallas as pl
from jax.experimental.pallas import tpu as pltpu
from jax.sharding import PartitionSpec as P

SWEEPS = 3
MESH = pl.DeviceIdType.MESH


def loop(count, body, init, unroll=4):
    if count % unroll:
        unroll = 1

    def outer(step, carry):
        for part in range(unroll):
            carry = body(step * unroll + part, carry)
        return carry

    return lax.fori_loop(0, count // unroll, outer, init)


def later(count, body, init, unroll=5):
    return loop(count - 1, lambda step, carry: body(step + 1, carry), init, unroll)


def mat_vec(matrix, vector):
    return [
        matrix[3 * a] * vector[0] + matrix[3 * a + 1] * vector[1] + matrix[3 * a + 2] * vector[2]
        for a in range(3)
    ]


def mat_mat(left, right):
    return [
        left[3 * a] * right[b] + left[3 * a + 1] * right[3 + b] + left[3 * a + 2] * right[6 + b]
        for a in range(3)
        for b in range(3)
    ]


def added(left, right):
    return [a + b for a, b in zip(left, right)]


def planes(ref, index, count=3):
    return [ref[index, c] for c in range(count)]


def put(ref, index, values):
    for c, value in enumerate(values):
        ref[index, c] = value


def kernel(
    surf_size,
    norm_size,
    amplitude,
    mode_patch,
    column_patch,
    wall_mask,
    offsets,
    modes_hbm,
    coupling_hbm,
    pivot_hbm,
    stiffness_hbm,
    out,
    modes,
    coupling,
    pivot,
    stiffness,
    link,
    link_next,
    maps,
    end_map,
    part,
    got,
    mask_edge,
    wall,
    values,
    enter,
    edge_out,
    edge_in,
    halo,
    f_in,
    f_out,
    o_in,
    o_out,
    h_in,
    h_out,
    up_in,
    up_out,
    down_in,
    down_out,
    load_sem,
    part_send,
    part_recv,
    mask_send,
    mask_recv,
    link_send,
    link_recv,
    h_send,
    h_recv,
    up_send,
    up_recv,
    down_send,
    down_recv,
    f_send,
    f_recv,
    o_send,
    o_recv,
    edge_send,
    edge_recv,
):
    S, N = surf_size, norm_size
    K, _, R, W = pivot.shape
    M = modes.shape[0]
    B = 2 * R
    blocks = modes.shape[2] // B
    me = lax.axis_index("surf")
    place = lax.axis_index("norm")
    before = lax.rem(me + S - 1, S)
    after = lax.rem(me + 1, S)
    first, last = place == 0, place == N - 1

    def to_surf(src, dst, send, recv, target):
        return pltpu.make_async_remote_copy(
            src_ref=src, dst_ref=dst, send_sem=send, recv_sem=recv,
            device_id={"surf": target}, device_id_type=MESH,
        )

    def to_norm(src, dst, send, recv, target):
        return pltpu.make_async_remote_copy(
            src_ref=src, dst_ref=dst, send_sem=send, recv_sem=recv,
            device_id={"norm": target}, device_id_type=MESH,
        )

    mode_loads = [
        pltpu.make_async_copy(
            modes_hbm.at[:, :, pl.ds(b * B, B), :], modes.at[:, :, pl.ds(b * B, B), :], load_sem.at[3 + b]
        )
        for b in range(blocks)
    ]
    loads = [
        pltpu.make_async_copy(coupling_hbm, coupling, load_sem.at[0]),
        pltpu.make_async_copy(pivot_hbm, pivot, load_sem.at[1]),
        pltpu.make_async_copy(stiffness_hbm, stiffness, load_sem.at[2]),
    ]
    for copy in mode_loads + loads:
        copy.start()

    barrier = pltpu.get_barrier_semaphore()
    for hop in range(1, S):
        pl.semaphore_signal(
            barrier, inc=1, device_id={"surf": lax.rem(me + hop, S)}, device_id_type=MESH
        )

    for hop in range(1, N):
        pl.semaphore_signal(
            barrier, inc=1, device_id={"norm": lax.rem(place + hop, N)}, device_id_type=MESH
        )

    own_mode = me * M
    for b in range(blocks):
        mode_loads[b].wait()
        patch = column_patch[b * B : (b + 1) * B, :]

        def mode_step(m, sums):
            weight = jnp.where(
                patch == mode_patch[own_mode + m], amplitude[own_mode + m], jnp.float32(0)
            )
            return [
                sums[c] + weight * modes[m, c, b * B : (b + 1) * B, :].astype(jnp.float32)
                for c in range(3)
            ]

        sums = loop(M, mode_step, [jnp.zeros((B, W), jnp.float32)] * 3)
        for c in range(3):
            for side in range(2):
                dest = 2 * b + side
                block = sums[c][side * R : (side + 1) * R]
                part[dest, c] = block
                part[(dest + 1) % S, 3, c : c + 1, :] = block[R - 1 : R]
                part[(dest - 1) % S, 3, 3 + c : 4 + c, :] = block[0:1]

    pl.semaphore_wait(barrier, S + N - 2)

    def part_copy(hop):
        dest = lax.rem(me + hop, S)
        return to_surf(part.at[dest], got.at[hop], part_send.at[hop], part_recv.at[hop], dest)

    for hop in range(1, S):
        part_copy(hop).start()
    mask_up = to_surf(wall_mask, mask_edge.at[0], mask_send.at[0], mask_recv.at[0], after)
    mask_down = to_surf(wall_mask, mask_edge.at[1], mask_send.at[1], mask_recv.at[1], before)
    mask_up.start()
    mask_down.start()
    link_copy = to_norm(coupling_hbm.at[0], link_next, link_send, link_recv, place - 1)

    @pl.when(jnp.logical_not(first))
    def _():
        link_copy.start()

    for copy in loads:
        copy.wait()
    cut = offsets[...]
    base = place * K

    def link_step(k, carry):
        link[k] = jnp.where(cut == base + k, jnp.float32(0), coupling[k])
        return carry

    loop(K, link_step, 0)

    @pl.when(last)
    def _():
        link[K] = jnp.zeros((R, W), jnp.float32)

    def lower_step(k, state):
        scaled = [p * link[k] for p in planes(pivot, k, 9)]
        state = mat_mat(scaled, state)
        put(maps, k, state)
        return state

    first_map = [p * link[0] for p in planes(pivot, 0, 9)]
    put(maps, 0, first_map)
    ends = lax.fori_loop(1, K, lower_step, first_map)
    for c in range(9):
        end_map[c] = ends[c]

    @pl.when(jnp.logical_not(last))
    def _():
        link_copy.wait_recv()
        link[K] = jnp.where(cut == base + K, jnp.float32(0), link_next[...])

    def upper_step(step, state):
        k = K - 1 - step
        scaled = [p * link[k + 1] for p in planes(pivot, k, 9)]
        state = added(planes(maps, k, 9), mat_mat(scaled, state[:9])) + mat_mat(scaled, state[9:])
        put(maps, k, state)
        return state

    top_link = link[K]
    top_state = planes(maps, K - 1, 9) + [p * top_link for p in planes(pivot, K - 1, 9)]
    put(maps, K - 1, top_state)
    top_state = lax.fori_loop(1, K, upper_step, top_state)

    h_copy = to_norm(h_out, h_in, h_send, h_recv, place - 1)
    inside = jnp.logical_not(jnp.logical_or(first, last))

    def up_map(j):
        return to_norm(up_out.at[j], up_in.at[j], up_send.at[j], up_recv.at[j], place + 1)

    def down_map(j):
        return to_norm(down_out.at[j], down_in.at[j], down_send.at[j], down_recv.at[j], place - 1)

    def sends_up(j):
        return jnp.logical_and(place >= j, jnp.logical_not(last))

    def sends_down(j):
        return jnp.logical_and(N - 1 - place >= j, jnp.logical_not(first))

    @pl.when(last)
    def _():
        h_in[...] = jnp.zeros((9, R, W), jnp.float32)
        for c in range(9):
            h_out[c] = maps[0, c]
        h_copy.start()

    for j in range(1, min(2, N - 1)):

        @pl.when(sends_up(j))
        def _():
            put(up_out, j, [end_map[c] for c in range(9)])
            up_map(j).start()

        @pl.when(sends_down(j))
        def _():
            put(down_out, j, [maps[0, 9 + c] for c in range(9)])
            down_map(j).start()

    @pl.when(inside)
    def _():
        h_copy.wait_recv()
        inner = mat_mat([h_in[c] for c in range(9)], [end_map[c] for c in range(9)])
        whole = added(planes(maps, 0, 9), mat_mat([maps[0, 9 + c] for c in range(9)], inner))
        for c in range(9):
            h_out[c] = whole[c]
        h_copy.start()

    for j in range(2, N):

        @pl.when(place >= j)
        def _():
            up_map(j - 1).wait_recv()

        @pl.when(N - 1 - place >= j)
        def _():
            down_map(j - 1).wait_recv()

        if j < N - 1:

            @pl.when(sends_up(j))
            def _():
                put(up_out, j, mat_mat([end_map[c] for c in range(9)], planes(up_in, j - 1, 9)))
                up_map(j).start()

            @pl.when(sends_down(j))
            def _():
                put(
                    down_out, j,
                    mat_mat([maps[0, 9 + c] for c in range(9)], planes(down_in, j - 1, 9)),
                )
                down_map(j).start()

    total = [part[me, c] for c in range(4)]
    mask_up.wait_recv()
    mask_down.wait_recv()
    for hop in range(1, S):
        part_copy(hop).wait_recv()
        total = [total[c] + got[hop, c] for c in range(4)]
    mask = wall_mask[...].astype(jnp.float32)
    low_mask = mask_edge[0, R - 1 : R, :].astype(jnp.float32)
    high_mask = mask_edge[1, 0:1, :].astype(jnp.float32)
    row = lax.broadcasted_iota(jnp.int32, (R, W), 0)
    lane = lax.broadcasted_iota(jnp.int32, (R, W), 1)

    def around(x, low, high):
        nearby = jnp.where(row == 0, low, pltpu.roll(x, 1, 0))
        nearby += jnp.where(row == R - 1, high, pltpu.roll(x, R - 1, 0))
        nearby += jnp.where(lane == 0, jnp.float32(0), pltpu.roll(x, 1, 1))
        return nearby + jnp.where(lane == W - 1, jnp.float32(0), pltpu.roll(x, W - 1, 1))

    at_wall = jnp.where(first, jnp.float32(1), jnp.float32(0))
    for c in range(3):
        shift = total[c] * mask
        wall[c] = link[0] * shift * at_wall
        wall[3 + c] = around(
            shift, total[3][c : c + 1] * low_mask, total[3][3 + c : 4 + c] * high_mask
        )

    def edge_copies(sweep):
        return [
            to_surf(edge_out.at[sweep, 1], edge_in.at[sweep, 0], edge_send.at[sweep, 0], edge_recv.at[sweep, 0], after),
            to_surf(edge_out.at[sweep, 0], edge_in.at[sweep, 1], edge_send.at[sweep, 1], edge_recv.at[sweep, 1], before),
        ]

    def up_copy(sweep, j):
        return to_norm(
            f_out.at[sweep], f_in.at[sweep, j], f_send.at[sweep, j], f_recv.at[sweep, j], place + j
        )

    def down_copy(sweep, j):
        return to_norm(
            o_out.at[sweep], o_in.at[sweep, j], o_send.at[sweep, j], o_recv.at[sweep, j], place - j
        )

    for sweep in range(SWEEPS):
        if sweep > 0:
            for copy in edge_copies(sweep - 1):
                copy.wait_recv()
            for side in range(2):
                halo[side] = edge_in[sweep - 1, side].astype(jnp.float32)

        def source(k, sweep=sweep):
            if sweep == 0:
                blend = 1.0 - (base + k).astype(jnp.float32) / (K * N)
                factor = stiffness[k] * blend
                return [factor * wall[3 + c] for c in range(3)]
            return [
                stiffness[k]
                * around(out[k, c], halo[0, c, pl.ds(k, 1), :], halo[1, c, pl.ds(k, 1), :])
                for c in range(3)
            ]

        def forward(k, state):
            right = added(source(k), [link[k] * s for s in state])
            state = mat_vec(planes(pivot, k, 9), right)
            put(values, k, state)
            return state

        start = mat_vec(
            planes(pivot, 0, 9), added(source(0), [wall[c] for c in range(3)])
        )
        put(values, 0, start)
        ends = later(K, forward, start)

        def backward(step, state):
            k = K - 1 - step
            state = added(
                planes(values, k), mat_vec(planes(pivot, k, 9), [link[k + 1] * s for s in state])
            )
            put(values, k, state)
            return state

        tops = later(K, backward, ends)
        put(f_out, sweep, ends)
        for j in range(N - 1, 0, -1):

            @pl.when(place + j < N)
            def _():
                up_copy(sweep, j).start()

        if sweep == 0:

            @pl.when(first)
            def _():
                h_copy.wait_recv()

        @pl.when(jnp.logical_not(first))
        def _():
            top = added(
                tops,
                mat_vec(
                    [maps[0, 9 + c] for c in range(9)], mat_vec([h_in[c] for c in range(9)], ends)
                ),
            )
            put(o_out, sweep, top)
            for j in range(N - 1, 0, -1):

                @pl.when(place - j >= 0)
                def _():
                    down_copy(sweep, j).start()

        enter[...] = jnp.zeros(enter.shape, jnp.float32)
        for j in range(1, N):

            @pl.when(place - j >= 0)
            def _():
                up_copy(sweep, j).wait_recv()
                moved = planes(f_in.at[sweep], j)
                if j > 1:
                    moved = mat_vec(planes(up_in, j - 1, 9), moved)
                put(enter, 0, added(planes(enter, 0), moved))

            @pl.when(place + j < N)
            def _():
                down_copy(sweep, j).wait_recv()
                moved = planes(o_in.at[sweep], j)
                if j > 1:
                    moved = mat_vec(planes(down_in, j - 1, 9), moved)
                put(enter, 1, added(planes(enter, 1), moved))

        entering = planes(enter, 0)
        state = added(ends, mat_vec([end_map[c] for c in range(9)], entering))
        above = added(planes(enter, 1), mat_vec([h_in[c] for c in range(9)], state))

        def finish(k, carry, sweep=sweep):
            state = added(planes(values, k), mat_vec(planes(maps, k, 9), entering))
            state = added(state, mat_vec([maps[k, 9 + c] for c in range(9)], above))
            put(out, k, state)
            if sweep < SWEEPS - 1:
                for c in range(3):
                    halo[0, c, pl.ds(k, 1), :] = state[c][0:1]
                    halo[1, c, pl.ds(k, 1), :] = state[c][R - 1 : R]
            return carry

        loop(K, finish, 0, 4)
        if sweep < SWEEPS - 1:
            for side in range(2):
                edge_out[sweep, side] = halo[side].astype(jnp.bfloat16)
            for copy in edge_copies(sweep):
                copy.start()

    for hop in range(1, S):
        part_copy(hop).wait_send()
    mask_up.wait_send()
    mask_down.wait_send()
    for sweep in range(SWEEPS - 1):
        for copy in edge_copies(sweep):
            copy.wait_send()

    @pl.when(jnp.logical_not(first))
    def _():
        link_copy.wait_send()
        h_copy.wait_send()

    for j in range(1, N):
        if j < N - 1:

            @pl.when(sends_up(j))
            def _():
                up_map(j).wait_send()

            @pl.when(sends_down(j))
            def _():
                down_map(j).wait_send()

        for sweep in range(SWEEPS):

            @pl.when(place + j < N)
            def _():
                up_copy(sweep, j).wait_send()

            @pl.when(place - j >= 0)
            def _():
                down_copy(sweep, j).wait_send()


def per_device(
    surf_size, norm_size, mode_shapes, amplitude, mode_patch, column_patch, wall_mask, offsets,
    coupling, pivot_inv, stiffness,
):
    S, N = surf_size, norm_size
    modes = mode_shapes.transpose(0, 2, 1, 3)
    pivot = pivot_inv.transpose(0, 2, 1, 3)
    K, _, R, W = pivot.shape
    f32, bf16 = jnp.float32, jnp.bfloat16
    vmem = pl.BlockSpec(memory_space=pltpu.VMEM)
    smem = pl.BlockSpec(memory_space=pltpu.SMEM)
    hbm = pl.BlockSpec(memory_space=pl.ANY)
    dma = pltpu.SemaphoreType.DMA
    out = pl.pallas_call(
        functools.partial(kernel, surf_size, norm_size),
        out_shape=jax.ShapeDtypeStruct((K, 3, R, W), f32),
        in_specs=[smem, smem, vmem, vmem, vmem, hbm, hbm, hbm, hbm],
        out_specs=vmem,
        scratch_shapes=[
            pltpu.VMEM(modes.shape, bf16),
            pltpu.VMEM((K, R, W), f32),
            pltpu.VMEM((K, 9, R, W), f32),
            pltpu.VMEM((K, R, W), f32),
            pltpu.VMEM((K + 1, R, W), f32),
            pltpu.VMEM((R, W), f32),
            pltpu.VMEM((K, 18, R, W), f32),
            pltpu.VMEM((9, R, W), f32),
            pltpu.VMEM((S, 4, R, W), f32),
            pltpu.VMEM((S, 4, R, W), f32),
            pltpu.VMEM((2, R, W), jnp.int32),
            pltpu.VMEM((6, R, W), f32),
            pltpu.VMEM((K, 3, R, W), f32),
            pltpu.VMEM((2, 3, R, W), f32),
            pltpu.VMEM((SWEEPS - 1, 2, 3, K, W), bf16),
            pltpu.VMEM((SWEEPS - 1, 2, 3, K, W), bf16),
            pltpu.VMEM((2, 3, K, W), f32),
            pltpu.VMEM((SWEEPS, N, 3, R, W), f32),
            pltpu.VMEM((SWEEPS, 3, R, W), f32),
            pltpu.VMEM((SWEEPS, N, 3, R, W), f32),
            pltpu.VMEM((SWEEPS, 3, R, W), f32),
            pltpu.VMEM((9, R, W), f32),
            pltpu.VMEM((9, R, W), f32),
            pltpu.VMEM((N, 9, R, W), f32),
            pltpu.VMEM((N, 9, R, W), f32),
            pltpu.VMEM((N, 9, R, W), f32),
            pltpu.VMEM((N, 9, R, W), f32),
            dma((3 + modes.shape[2] // (2 * R),)),
            dma((S,)),
            dma((S,)),
            dma((2,)),
            dma((2,)),
            dma,
            dma,
            dma,
            dma,
            dma((N,)),
            dma((N,)),
            dma((N,)),
            dma((N,)),
            dma((SWEEPS, N)),
            dma((SWEEPS, N)),
            dma((SWEEPS, N)),
            dma((SWEEPS, N)),
            dma((SWEEPS - 1, 2)),
            dma((SWEEPS - 1, 2)),
        ],
        compiler_params=pltpu.CompilerParams(collective_id=0, has_side_effects=True),
        name="line_sweeps",
    )(amplitude, mode_patch, column_patch, wall_mask, offsets, modes, coupling, pivot, stiffness)
    return out.transpose(0, 2, 1, 3)


def solution(mesh):
    return jax.shard_map(
        functools.partial(per_device, mesh.shape["surf"], mesh.shape["norm"]),
        mesh=mesh,
        in_specs=(
            P("surf", None, None, None),
            P(),
            P(),
            P(),
            P("surf", None),
            P("surf", None),
            P("norm", "surf", None),
            P("norm", "surf", None, None),
            P("norm", "surf", None),
        ),
        out_specs=P("norm", "surf", None, None),
        check_vma=False,
    )
```
